128 devices in a mesh: seq: 32 (over x, z, core), tp: 4 (over y).
Axes of the slice: x: 4, y: 4, z: 4, core: 2. Of those that a mesh axis runs over, the one named last changes fastest.
Arguments:
- hidden: bfloat16 [384, 1024], P('seq'), may hold values from -60 to 60
- norm_gains: float32 [3, 1024], replicated, may hold values from 0.5 to 1.5
- w_qkv: bfloat16 [3, 1024, 1024], P(None, None, 'tp'), may hold values from -0.1875 to 0.1875
- w_self_out: bfloat16 [1024, 1024], P('tp'), may hold values from -0.1875 to 0.1875
- w_cross_q: bfloat16 [1024, 1024], P(None, 'tp'), may hold values from -0.1875 to 0.1875
- w_cross_out: bfloat16 [1024, 1024], P('tp'), may hold values from -0.1875 to 0.1875
- w_up: bfloat16 [1024, 8192], P(None, 'tp'), may hold values from -0.1875 to 0.1875
- w_down: bfloat16 [8192, 1024], P('tp'), may hold values from -0.0625 to 0.0625
- kv_cache: bfloat16 [2, 3072, 128, 1024], P(None, 'seq', None, 'tp'), may hold values from -70 to 70
- encoder_kv: bfloat16 [2, 96, 256, 1024], P(None, 'seq', None, 'tp'), may hold values from -70 to 70
- cache_lengths: int32 [96], replicated, may hold values from 129 to 65536, as said below
- page_table: int32 [96, 512], replicated, may hold values from -1 to 3071, as said below
- group_of: int32 [96], replicated, may hold values from 0 to 11, as said below
Outputs:
- updated: bfloat16 [384, 1024], P('seq', 'tp')
The draws below stay inside these ranges and needn't reach their ends.
Inputs may be any that keep to these rules, and one draw needn't show every extreme that they name: `group_of`: each of the 12 groups holds exactly 8 requests. Request r has ceil(cache_lengths[r] / 128) pages in page_table, every one full but its last; some request has exactly 65536 positions. `page_table`: entry [r, j] is the global slot (device index along seq times 96 plus local slot) of request r's page j, or -1 past its last page. The requests of one group begin with the same full pages (their prompt); their other pages are their own. No slot serves two groups. On every device the used slots are its first ones, and some device uses all 96.
All inputs are finite; a program needn't handle non-finite values.
Results may differ from the reference program's by a relative error of at most 0.005.
The reference program's roundings to bfloat16 on the way count: a program that leaves them out, or rounds other values in their place, can miss the bound.
Values may be sent and summed in bfloat16 or wider, within the bound.
A program may use at most 128 MiB of HBM per device.

```python
import math
import jax
import jax.numpy as jnp
from jax import lax

D = 1024
H = 16
HD = 64
FF = 8192
PAGE = 128
MAX_PAGES = 512
NEW = 4
GSIZE = 8
P_DEV = 96
SRC = 256
R = 96
GROUPS = 12
ROWS = 384
PAGES = 3072
N_SEQ = 32


def cache_layout(key):
    streams = jax.random.split(jax.random.fold_in(key, 11), 7)
    shuffled = jax.random.permutation(streams[0], R).astype(jnp.int32)
    group_ids = (shuffled // GSIZE).astype(jnp.int32)
    spare_pages = PAGES - MAX_PAGES - R - GROUPS
    extra_prompt = min(spare_pages // (2 * GROUPS), MAX_PAGES // 2)
    extra_own = spare_pages // (2 * R)
    prompt_pages = 1 + jax.random.randint(streams[1], (GROUPS,), 0, extra_prompt + 1, dtype=jnp.int32)
    own_pages = 1 + jax.random.randint(streams[2], (R,), 0, extra_own + 1, dtype=jnp.int32)
    longest = jax.random.randint(streams[3], (), 0, R, dtype=jnp.int32)
    request_ids = jnp.arange(R, dtype=jnp.int32)
    prompt_of = prompt_pages[group_ids]
    own_pages = jnp.minimum(own_pages, MAX_PAGES - prompt_of)
    own_pages = jnp.where(request_ids == longest, MAX_PAGES - prompt_of, own_pages)
    last_fill = jax.random.randint(streams[4], (R,), 1, PAGE + 1, dtype=jnp.int32)
    last_fill = jnp.where(request_ids == longest, PAGE, last_fill)
    lengths = (prompt_of + own_pages - 1) * PAGE + last_fill
    device_weight = jax.random.randint(streams[5], (N_SEQ,), 1, 5, dtype=jnp.int32)
    full_device = jax.random.randint(streams[6], (), 0, N_SEQ, dtype=jnp.int32)
    device_ids = jnp.arange(N_SEQ, dtype=jnp.int32)
    device_weight = jnp.where(device_ids == full_device, 0, device_weight)
    slot_ids = jnp.arange(P_DEV, dtype=jnp.int32)[None, :]
    priority = (slot_ids + 1) * device_weight[:, None] * PAGES + slot_ids * N_SEQ + device_ids[:, None]
    placement_order = jnp.argsort(priority.reshape(-1), stable=True).astype(jnp.int32)
    prompt_start = jnp.cumsum(prompt_pages) - prompt_pages
    prompt_total = jnp.sum(prompt_pages)
    own_start = jnp.cumsum(own_pages) - own_pages
    column = jnp.arange(MAX_PAGES, dtype=jnp.int32)[None, :]
    prompt_here = prompt_of[:, None]
    page_item = jnp.where(column < prompt_here, prompt_start[group_ids][:, None] + column, prompt_total + own_start[:, None] + column - prompt_here)
    page_used = column < prompt_here + own_pages[:, None]
    table = jnp.where(page_used, placement_order[jnp.clip(page_item, 0, PAGES - 1)], -1)
    return (group_ids, lengths.astype(jnp.int32), table.astype(jnp.int32))


def draw_group_of(key, part):
    return cache_layout(key)[0]


def draw_cache_lengths(key, part):
    return cache_layout(key)[1]


def draw_page_table(key, part):
    return cache_layout(key)[2]


def draw_hidden(key, part):
    streams = jax.random.split(jax.random.fold_in(key, 3), 3)
    row_scale = jnp.exp(jax.random.uniform(streams[0], (ROWS, 1), jnp.float32, math.log(0.3), math.log(3.0)))
    col_scale = jnp.exp(jax.random.uniform(streams[1], (1, D), jnp.float32, math.log(0.3), math.log(3.0)))
    values = jnp.clip(jax.random.normal(streams[2], (ROWS, D), jnp.float32), -6.0, 6.0) * row_scale * col_scale
    return values.astype(jnp.bfloat16)


def draw_kv_cache(key, part):
    streams = jax.random.split(jax.random.fold_in(key, 5), 1)
    values = jnp.clip(jax.random.normal(streams[0], (2, PAGES, PAGE, D), jnp.float32), -6.0, 6.0)
    return values.astype(jnp.bfloat16)


def draw_encoder_kv(key, part):
    streams = jax.random.split(jax.random.fold_in(key, 9), 1)
    values = jnp.clip(jax.random.normal(streams[0], (2, R, SRC, D), jnp.float32), -6.0, 6.0)
    return values.astype(jnp.bfloat16)


def steps_of(key, shape, pieces, least, high):
    loudness = 1.0
    for axis_at, shards_of in pieces:
        heights = jax.random.uniform(jax.random.fold_in(jax.random.fold_in(key, 6), axis_at), (shards_of,), jnp.float32, least / len(pieces), high / len(pieces))
        loudness = loudness * jnp.repeat(jnp.exp(heights), shape[axis_at] // shards_of).reshape((-1,) + (1,) * (len(shape) - 1 - axis_at))
    return loudness


def normal_values(stream_key, extent, deviation, limit, cuts=(), kind=jnp.bfloat16):
    gain = steps_of(stream_key, extent, cuts, -0.22, 0.18) if cuts else 1.0
    array = jax.random.normal(stream_key, extent, jnp.float32) * deviation * gain
    return jnp.minimum(jnp.maximum(array, -limit), limit).astype(kind)


def setup_inputs(seed: int = 0) -> dict:
    key_list = jax.random.split(jax.random.key(seed), 14)
    hidden = draw_hidden(jax.random.fold_in(key_list[13], 71), 0)
    norm_gains = jnp.clip(1.0 + 0.1 * jax.random.normal(key_list[1], (3, D), jnp.float32), 0.5, 1.5)
    w_qkv = normal_values(key_list[2], (3, D, D), D ** -0.5, 0.1875, ((2, 4),))
    w_self_out = normal_values(key_list[3], (D, D), D ** -0.5, 0.1875, ((0, 4),))
    w_cross_q = normal_values(key_list[4], (D, D), D ** -0.5, 0.1875, ((1, 4),))
    w_cross_out = normal_values(key_list[5], (D, D), D ** -0.5, 0.1875, ((0, 4),))
    w_up = normal_values(key_list[6], (D, FF), D ** -0.5, 0.1875, ((1, 4),))
    w_down = normal_values(key_list[7], (FF, D), FF ** -0.5, 0.0625, ((0, 4),))
    kv_cache = draw_kv_cache(jax.random.fold_in(key_list[13], 71), 0)
    encoder_kv = draw_encoder_kv(jax.random.fold_in(key_list[13], 71), 0)
    cache_lengths = draw_cache_lengths(jax.random.fold_in(key_list[13], 71), 0)
    page_table = draw_page_table(jax.random.fold_in(key_list[13], 71), 0)
    group_of = draw_group_of(jax.random.fold_in(key_list[13], 71), 0)
    return dict(hidden=hidden, norm_gains=norm_gains, w_qkv=w_qkv, w_self_out=w_self_out, w_cross_q=w_cross_q, w_cross_out=w_cross_out, w_up=w_up, w_down=w_down, kv_cache=kv_cache, encoder_kv=encoder_kv, cache_lengths=cache_lengths, page_table=page_table, group_of=group_of)


NEG_BIG = -1e+30

def to_bf16(values):
    return lax.optimization_barrier(values.astype(jnp.bfloat16))

def layer_norm(values, norm_gain):
    centre = values - lax.optimization_barrier(jnp.mean(values, axis=-1, keepdims=True))
    spread = lax.optimization_barrier(jnp.mean(centre * centre, axis=-1, keepdims=True))
    return centre * lax.rsqrt(spread + 1e-05) * norm_gain

def page_meta(page_table, group_of, cache_lengths, first_slot, slot_count, page_len, group_size):
    request_count, most_pages = page_table.shape
    flat_table = page_table.reshape(-1)
    logical = jnp.tile(jnp.arange(most_pages, dtype=jnp.int32), request_count)
    owner_ids = jnp.repeat(jnp.arange(request_count, dtype=jnp.int32), most_pages)
    local_slot = flat_table - first_slot
    inside = (flat_table >= 0) & (local_slot >= 0) & (local_slot < slot_count)
    target = jnp.where(inside, local_slot, slot_count).astype(jnp.int32)
    slot_page = jnp.zeros((slot_count + 1,), jnp.int32).at[target].max(logical)[:slot_count]
    slot_group = jnp.zeros((slot_count + 1,), jnp.int32).at[target].max(group_of[owner_ids])[:slot_count]
    in_use = jnp.zeros((slot_count + 1,), jnp.int32).at[target].max(jnp.ones_like(target))[:slot_count]
    members = jnp.argsort(group_of, stable=True).astype(jnp.int32).reshape(request_count // group_size, group_size)
    slot_members = members[slot_group]
    global_page = first_slot + jnp.arange(slot_count, dtype=jnp.int32)
    owned_page = page_table[slot_members, slot_page[:, None]] == global_page[:, None]
    position = slot_page[:, None] * page_len + jnp.arange(page_len, dtype=jnp.int32)[None, :]
    valid_keys = owned_page[:, :, None] & (position[:, None, :] < cache_lengths[slot_members][:, :, None])
    return (slot_members, valid_keys, jnp.sum(in_use))

def fold_parts(running, peak_score, weight_sum, weighted, row_index, head_count):
    old_peak, old_sum, old_acc = running
    new_peak = old_peak.at[row_index].max(peak_score)
    keep_factor = jnp.exp(old_peak - new_peak)
    factor = jnp.exp(peak_score - new_peak[row_index])
    new_sum = (old_sum * keep_factor).at[row_index].add(weight_sum * factor)
    head_width = old_acc.shape[1] // head_count
    scaled_acc = old_acc.reshape(-1, head_count, head_width) * keep_factor[:, :, None]
    new_acc = scaled_acc.at[row_index].add(weighted * factor[:, :, None]).reshape(-1, head_count * head_width)
    return (new_peak, new_sum, new_acc)

def page_block(running, page_keys, page_values, query_heads, slot_members, valid_keys):
    new_count = query_heads.shape[1]
    head_count = query_heads.shape[2]
    picked = query_heads[slot_members]
    scores = jnp.einsum('sgthe,skhe->sgthk', picked.astype(jnp.float32), page_keys.astype(jnp.float32)) * HD ** (-0.5)
    key_mask = valid_keys[:, :, None, None, :]
    scores = jnp.where(key_mask, scores, NEG_BIG)
    peak_score = lax.optimization_barrier(jnp.max(scores, axis=-1))
    exponent = jnp.where(key_mask, jnp.exp(scores - peak_score[..., None]), 0.0)
    weight_sum = lax.optimization_barrier(jnp.sum(exponent, axis=-1))
    rounded = to_bf16(exponent)
    weighted = jnp.einsum('sgthk,skhe->sgthe', rounded.astype(jnp.float32), page_values.astype(jnp.float32))
    row_index = (slot_members[:, :, None] * new_count + jnp.arange(new_count, dtype=jnp.int32)[None, None, :]).reshape(-1)
    return fold_parts(running, peak_score.reshape(-1, head_count), weight_sum.reshape(-1, head_count), weighted.reshape(-1, head_count, HD), row_index, head_count)

def fresh_part(query_heads, key_heads, value_heads):
    new_count = query_heads.shape[1]
    head_count = query_heads.shape[2]
    scores = jnp.einsum('rthe,ruhe->rthu', query_heads.astype(jnp.float32), key_heads.astype(jnp.float32)) * HD ** (-0.5)
    causal = (jnp.arange(new_count)[:, None] >= jnp.arange(new_count)[None, :])[None, :, None, :]
    scores = jnp.where(causal, scores, NEG_BIG)
    peak_score = lax.optimization_barrier(jnp.max(scores, axis=-1))
    exponent = jnp.where(causal, jnp.exp(scores - peak_score[..., None]), 0.0)
    weight_sum = lax.optimization_barrier(jnp.sum(exponent, axis=-1))
    rounded = to_bf16(exponent)
    weighted = jnp.einsum('rthu,ruhe->rthe', rounded.astype(jnp.float32), value_heads.astype(jnp.float32))
    return (peak_score.reshape(-1, head_count), weight_sum.reshape(-1, head_count), weighted.reshape(-1, head_count * HD))

def combine_parts(first_part, second_part):
    peak_one, sum_one, acc_one = first_part
    peak_two, sum_two, acc_two = second_part
    head_count = peak_one.shape[1]
    peak_score = jnp.maximum(peak_one, peak_two)
    factor_one = jnp.exp(peak_one - peak_score)
    factor_two = jnp.exp(peak_two - peak_score)
    weight_sum = sum_one * factor_one + sum_two * factor_two
    head_width = acc_one.shape[1] // head_count
    weighted = acc_one.reshape(-1, head_count, head_width) * factor_one[:, :, None] + acc_two.reshape(-1, head_count, head_width) * factor_two[:, :, None]
    return (peak_score, weight_sum, weighted.reshape(-1, head_count * head_width))

def reference(hidden, norm_gains, w_qkv, w_self_out, w_cross_q, w_cross_out, w_up, w_down, kv_cache, encoder_kv, cache_lengths, page_table, group_of):
    residual = hidden.astype(jnp.float32)
    normed = to_bf16(layer_norm(residual, norm_gains[0]))
    queries = to_bf16(jnp.dot(normed, w_qkv[0], preferred_element_type=jnp.float32))
    new_keys = to_bf16(jnp.dot(normed, w_qkv[1], preferred_element_type=jnp.float32))
    new_values = to_bf16(jnp.dot(normed, w_qkv[2], preferred_element_type=jnp.float32))
    query_heads = queries.reshape(R, NEW, H, HD)
    slot_members, valid_keys, live_pages = page_meta(page_table, group_of, cache_lengths, 0, PAGES, PAGE, GSIZE)
    page_span = 8 if PAGES % 8 == 0 else 4
    key_pages = kv_cache[0].reshape(PAGES, PAGE, H, HD)
    value_pages = kv_cache[1].reshape(PAGES, PAGE, H, HD)

    def scan_step(running, block_index):
        block_start = block_index * page_span
        result = page_block(running, lax.dynamic_slice_in_dim(key_pages, block_start, page_span, 0), lax.dynamic_slice_in_dim(value_pages, block_start, page_span, 0), query_heads, lax.dynamic_slice_in_dim(slot_members, block_start, page_span, 0), lax.dynamic_slice_in_dim(valid_keys, block_start, page_span, 0))
        return (result, None)
    start_state = (jnp.full((ROWS, H), NEG_BIG, jnp.float32), jnp.zeros((ROWS, H), jnp.float32), jnp.zeros((ROWS, D), jnp.float32))
    cached, _ = lax.scan(scan_step, start_state, jnp.arange(PAGES // page_span, dtype=jnp.int32))
    fresh = fresh_part(query_heads, new_keys.reshape(R, NEW, H, HD), new_values.reshape(R, NEW, H, HD))
    peak_score, weight_sum, weighted = combine_parts(cached, fresh)
    attended = to_bf16((weighted.reshape(ROWS, H, HD) / weight_sum[:, :, None]).reshape(ROWS, D))
    self_mixed = residual + jnp.dot(attended, w_self_out, preferred_element_type=jnp.float32)
    cross_normed = to_bf16(layer_norm(self_mixed, norm_gains[1]))
    cross_queries = to_bf16(jnp.dot(cross_normed, w_cross_q, preferred_element_type=jnp.float32)).reshape(R, NEW, H, HD)
    enc_keys = encoder_kv[0].reshape(R, SRC, H, HD)
    enc_values = encoder_kv[1].reshape(R, SRC, H, HD)
    cross_scores = jnp.einsum('rthe,rshe->rths', cross_queries.astype(jnp.float32), enc_keys.astype(jnp.float32)) * HD ** (-0.5)
    cross_peak = lax.optimization_barrier(jnp.max(cross_scores, axis=-1, keepdims=True))
    cross_exp = jnp.exp(cross_scores - cross_peak)
    cross_probs = to_bf16(cross_exp / lax.optimization_barrier(jnp.sum(cross_exp, axis=-1, keepdims=True)))
    context = jnp.einsum('rths,rshe->rthe', cross_probs.astype(jnp.float32), enc_values.astype(jnp.float32))
    context = to_bf16(context.reshape(ROWS, D))
    cross_mixed = self_mixed + jnp.dot(context, w_cross_out, preferred_element_type=jnp.float32)
    last_normed = to_bf16(layer_norm(cross_mixed, norm_gains[2]))
    hidden_units = to_bf16(jnp.maximum(jnp.dot(last_normed, w_up, preferred_element_type=jnp.float32), 0.0))
    return (cross_mixed + jnp.dot(hidden_units, w_down, preferred_element_type=jnp.float32)).astype(jnp.bfloat16)
```

```python
import functools

import jax
import jax.numpy as jnp
from jax import lax
from jax.experimental import pallas as pl
from jax.experimental.pallas import tpu as pltpu
from jax.sharding import PartitionSpec as P

HD = 64
PAGE = 128
NEW = 4
GSIZE = 8
BLOCK = 16
NEG_BIG = -1e30
FLOOR = -1e29
MESH = pl.DeviceIdType.MESH
F32 = jnp.float32
BF16 = jnp.bfloat16
NT = (((1,), (1,)), ((), ()))
TN = (((0,), (0,)), ((), ()))


def iota(shape, dim):
    return lax.broadcasted_iota(jnp.int32, shape, dim)


def dot(a, b, dims=None):
    if dims is None:
        return jnp.dot(a, b, preferred_element_type=F32)
    return lax.dot_general(a, b, dims, preferred_element_type=F32)


def layer_norm(values, gain):
    centre = values - jnp.mean(values, axis=-1, keepdims=True)
    spread = jnp.mean(centre * centre, axis=-1, keepdims=True)
    return (centre * lax.rsqrt(spread + 1e-05) * gain).astype(BF16)


def one_hot(condition):
    return jnp.where(condition, 1.0, 0.0).astype(BF16)


def kernel(
    n_seq,
    n_tp,
    hidden_h,
    gains_h,
    wqkv_h,
    wso_h,
    wcq_h,
    wco_h,
    wup_h,
    wdn_h,
    kv_h,
    enc_h,
    len_h,
    table_h,
    group_h,
    out_ref,
    hidden,
    gains,
    wqkv,
    wso,
    wcq,
    wco,
    wup,
    wdn,
    kbuf,
    vbuf,
    enc,
    lens,
    table,
    groups,
    resid,
    own,
    qall,
    table_t,
    nvalid_t,
    owners,
    nrh,
    gmat,
    scal_v,
    scal_s,
    to_dest,
    to_group,
    qbd,
    sbuf,
    mbuf,
    lbuf,
    mg,
    mparts,
    acc,
    mlsrc,
    paysrc,
    pay,
    got,
    tsend,
    trecv,
    dsend,
    drecv,
    load_sem,
    cache_sem,
    scal_sem,
    qsend_sem,
    qrecv_sem,
    psend_sem,
    precv_sem,
    tsend_sem,
    trecv_sem,
):
    own_rows, width = hidden.shape
    local = wso.shape[0]
    heads = local // HD
    slots = kbuf.shape[0]
    requests = groups.shape[1]
    group_count = requests // GSIZE
    own_requests = own_rows // NEW
    most_pages = table.shape[1]
    grows = GSIZE * NEW
    rh = heads * grows
    all_rows = n_seq * BLOCK
    sorted_rows = group_count * grows
    me = lax.axis_index("seq")
    my_tp = lax.axis_index("tp")

    loads = [
        (hidden_h, hidden),
        (gains_h, gains),
        (wqkv_h, wqkv),
        (table_h, table),
        (len_h, lens),
        (group_h, groups),
        (wso_h, wso),
        (wcq_h, wcq),
        (enc_h, enc),
        (wco_h, wco),
        (wup_h, wup),
        (wdn_h, wdn),
    ]
    copies = [
        pltpu.make_async_copy(src, dst, load_sem.at[i]) for i, (src, dst) in enumerate(loads)
    ]
    parts = 4
    span = slots // parts
    cache_copies = [
        pltpu.make_async_copy(
            kv_h.at[which, pl.ds(p * span, span)],
            buf.at[pl.ds(p * span, span)],
            cache_sem.at[which, p],
        )
        for which, buf in ((0, kbuf), (1, vbuf))
        for p in range(parts)
    ]
    for copy in copies[:6]:
        copy.start()

    barrier = pltpu.get_barrier_semaphore()

    def greet(k, carry):
        pl.semaphore_signal(
            barrier, inc=1, device_id={"seq": lax.rem(me + k, n_seq)}, device_id_type=MESH
        )
        return carry

    lax.fori_loop(1, n_seq, greet, 0)
    for k in range(1, n_tp):
        pl.semaphore_signal(
            barrier, inc=1, device_id={"tp": lax.rem(my_tp + k, n_tp)}, device_id_type=MESH
        )

    for copy in cache_copies[:parts]:
        copy.start()
    for copy in cache_copies[parts:]:
        copy.start()
    for copy in copies[6:]:
        copy.start()

    copies[0].wait()
    copies[1].wait()
    resid[...] = jnp.zeros_like(resid)
    resid[0:own_rows, :] = hidden[...].astype(F32)
    normed = layer_norm(resid[...], gains[0:1, :])
    copies[2].wait()
    queries = dot(normed, wqkv[0]).astype(BF16)
    qall[pl.ds(me * BLOCK, BLOCK), :] = queries
    own[0] = queries
    pl.semaphore_wait(barrier, n_seq + n_tp - 2)

    def query_copy(k, source):
        return pltpu.make_async_remote_copy(
            src_ref=own.at[0],
            dst_ref=qall.at[pl.ds(source * BLOCK, BLOCK), :],
            send_sem=qsend_sem.at[k],
            recv_sem=qrecv_sem.at[k],
            device_id={"seq": lax.rem(me + k, n_seq)},
            device_id_type=MESH,
        )

    def send_query(k, carry):
        query_copy(k, me).start()
        return carry

    lax.fori_loop(1, n_seq, send_query, 0)
    own[1] = dot(normed, wqkv[1]).astype(BF16)
    own[2] = dot(normed, wqkv[2]).astype(BF16)

    copies[3].wait()
    copies[4].wait()
    copies[5].wait()
    first_slot = me * slots
    eye = iota((requests, requests), 0) == iota((requests, requests), 1)
    group_row = groups[...]
    group_sq = jnp.broadcast_to(group_row, (requests, requests))
    group_col = jnp.sum(jnp.where(eye, group_sq, 0), axis=1, keepdims=True)
    earlier = iota((requests, requests), 0) < iota((requests, requests), 1)
    same = group_col == group_sq
    member_row = jnp.sum(jnp.where(same & earlier, 1, 0), axis=0, keepdims=True)
    member_sq = jnp.broadcast_to(member_row, (requests, requests))
    member_col = jnp.sum(jnp.where(eye, member_sq, 0), axis=1, keepdims=True)
    place_row = group_row * GSIZE + member_row
    place_col = group_col * GSIZE + member_col
    dest = iota((all_rows, requests), 0)
    inner = dest % BLOCK
    request_of = (dest // BLOCK) * own_requests + inner // NEW
    hit = (request_of == iota((all_rows, requests), 1)) & (inner < own_rows)
    at_col = jnp.sum(jnp.where(hit, place_row + 1, 0), axis=1, keepdims=True)
    token = iota((all_rows, 1), 0) % NEW
    at_col = jnp.where(at_col > 0, (at_col - 1) * NEW + token, -1)
    dest_t = iota((requests, all_rows), 1)
    inner_t = dest_t % BLOCK
    request_t = (dest_t // BLOCK) * own_requests + inner_t // NEW
    hit_t = (request_t == iota((requests, all_rows), 0)) & (inner_t < own_rows)
    at_row = jnp.sum(jnp.where(hit_t, place_col + 1, 0), axis=0, keepdims=True)
    token_t = iota((1, all_rows), 1) % NEW
    at_row = jnp.where(at_row > 0, (at_row - 1) * NEW + token_t, -1)
    to_dest[...] = one_hot(at_col == iota((all_rows, sorted_rows), 1))
    to_group[...] = one_hot(at_row == iota((sorted_rows, all_rows), 0))

    table_t[...] = jnp.transpose(table[...] - first_slot)
    page_at = iota((most_pages, requests), 0)
    nvalid_t[...] = jnp.clip(lens[...] - page_at * PAGE, 0, PAGE)
    unroll = 8

    def match(i, carry):
        slot0 = i * unroll

        def over_pages(j, sums):
            rows = pl.ds(pl.multiple_of(j * 8, 8), 8)
            at = table_t[rows, :]
            count = nvalid_t[rows, :]
            return tuple(jnp.where(at == slot0 + u, count, sums[u]) for u in range(unroll))

        sums = lax.fori_loop(
            0,
            most_pages // 8,
            over_pages,
            tuple(jnp.zeros((8, requests), jnp.int32) for _ in range(unroll)),
            unroll=4,
        )
        for u in range(unroll):
            owners[pl.ds(slot0 + u, 1), :] = jnp.max(sums[u], axis=0, keepdims=True)
        return carry

    lax.fori_loop(0, slots // unroll, match, 0)
    owner = owners[...]
    lane_member = (iota((requests, rh), 1) % grows) // NEW
    nrh[...] = dot(owner.astype(F32).astype(BF16), one_hot(member_col == lane_member))
    slot_group = jnp.max(jnp.where(owner > 0, group_row, -1), axis=1, keepdims=True)
    gmat[...] = jnp.broadcast_to(slot_group, (slots, rh))
    eye_s = iota((slots, slots), 0) == iota((slots, slots), 1)
    group_at = jnp.sum(
        jnp.where(eye_s, jnp.broadcast_to(slot_group, (slots, slots)), 0), axis=0, keepdims=True
    )
    before = (iota((slots, slots), 0) < iota((slots, slots), 1)) & (slot_group == group_at)
    before = before & (slot_group >= 0)
    previous = jnp.max(jnp.where(before, iota((slots, slots), 0), -1), axis=0, keepdims=True)
    mine = slot_group == iota((slots, 128), 1)
    last = jnp.max(jnp.where(mine, iota((slots, 128), 0), -1), axis=0, keepdims=True)
    scal_v[...] = jnp.zeros_like(scal_v)
    scal_v[0:1, 0:slots] = jnp.clip(group_at, 0, group_count - 1)
    scal_v[1:2, 0:slots] = jnp.where(previous < 0, slots, previous)
    scal_v[2:3, :] = jnp.where(last < 0, slots, last)
    scalars = pltpu.make_async_copy(scal_v, scal_s, scal_sem)
    scalars.start()

    def wait_query(k, carry):
        query_copy(k, lax.rem(me + n_seq - k, n_seq)).wait_recv()
        return carry

    lax.fori_loop(1, n_seq, wait_query, 0)
    sorted_queries = dot(to_group[...], qall[...]) * HD ** (-0.5)
    row_head = iota((grows, local), 1) // HD
    for g in range(group_count):
        block = sorted_queries[g * grows : (g + 1) * grows, :]
        for h in range(heads):
            qbd[g, h * grows : (h + 1) * grows, :] = jnp.where(row_head == h, block, 0.0).astype(
                BF16
            )
    scalars.wait()

    for copy in cache_copies[:parts]:
        copy.wait()
    key_at = iota((PAGE, rh), 0).astype(F32)
    step = 4

    def group_of_slot(s):
        return jnp.clip(scal_s[0, s], 0, group_count - 1)

    def acc_slot(row, at):
        return jnp.clip(scal_s[row, at], 0, slots)

    def score(i, carry):
        for u in range(step):
            s = i * step + u
            scores = dot(kbuf[s], qbd[group_of_slot(s)], NT)
            scores = jnp.where(key_at < nrh[pl.ds(s, 1), :], scores, NEG_BIG)
            sbuf[s] = scores
            mbuf[pl.ds(s, 1), :] = jnp.max(scores, axis=0, keepdims=True)
        return carry

    lax.fori_loop(0, slots // step, score, 0)
    for g in range(group_count):
        peak = jnp.max(jnp.where(gmat[...] == g, mbuf[...], NEG_BIG), axis=0, keepdims=True)
        peak = jnp.maximum(peak, FLOOR)
        high = peak.astype(BF16)
        low = (peak - high.astype(F32)).astype(BF16)
        mparts[0, g : g + 1, :] = high.astype(F32)
        mparts[1, g : g + 1, :] = low.astype(F32)
        mg[g] = jnp.broadcast_to(high.astype(F32) + low.astype(F32), (8, rh))

    for copy in cache_copies[parts:]:
        copy.wait()
    acc[slots] = jnp.zeros((grows, local), F32)

    def weigh(i, carry):
        for u in range(step):
            s = i * step + u
            peak = mg[group_of_slot(s)][0:1, :]
            weights = jnp.exp(sbuf[s] - peak)
            lbuf[pl.ds(s, 1), :] = jnp.sum(weights, axis=0, keepdims=True)
            product = dot(weights.astype(BF16), vbuf[s], TN)
            picked = product[0:grows, :]
            for h in range(1, heads):
                picked = jnp.where(row_head == h, product[h * grows : (h + 1) * grows, :], picked)
            acc[s] = picked + acc[acc_slot(1, s)]
        return carry

    lax.fori_loop(0, slots // step, weigh, 0)

    diagonal = (iota((grows, rh), 1) % grows) == iota((grows, rh), 0)
    for g in range(group_count):
        rows = slice(g * grows, (g + 1) * grows)
        total = jnp.sum(jnp.where(gmat[...] == g, lbuf[...], 0.0), axis=0, keepdims=True)
        high = total.astype(BF16).astype(F32)
        pieces = (mparts[0, g : g + 1, :], mparts[1, g : g + 1, :], high, total - high)
        for p, piece in enumerate(pieces):
            mlsrc[rows, p * rh : (p + 1) * rh] = jnp.where(diagonal, piece, 0.0).astype(BF16)
        paysrc[rows, 0:local] = acc[acc_slot(2, g)].astype(BF16)
    source = iota((4 * rh, 128), 0)
    spread = one_hot(
        iota((4 * rh, 128), 1) == (source // rh) * heads + (source % rh) // grows
    )
    paysrc[:, local:] = dot(mlsrc[...], spread).astype(BF16)
    pay[...] = dot(to_dest[...], paysrc[...]).astype(BF16)
    got[pl.ds(me * BLOCK, BLOCK), :] = pay[pl.ds(me * BLOCK, BLOCK), :]

    def part_copy(k, target, source):
        return pltpu.make_async_remote_copy(
            src_ref=pay.at[pl.ds(target * BLOCK, BLOCK), :],
            dst_ref=got.at[pl.ds(source * BLOCK, BLOCK), :],
            send_sem=psend_sem.at[k],
            recv_sem=precv_sem.at[k],
            device_id={"seq": target},
            device_id_type=MESH,
        )

    def send_part(k, carry):
        part_copy(k, lax.rem(me + k, n_seq), me).start()
        return carry

    lax.fori_loop(1, n_seq, send_part, 0)

    q_new = own[0].astype(F32) * HD ** (-0.5)
    k_new = own[1].astype(F32)
    v_new = own[2].astype(F32)
    same_head = one_hot(iota((local, local), 0) // HD == iota((local, local), 1) // HD)
    product = jnp.concatenate(
        [q_new * (pltpu.roll(k_new, d, 0) if d else k_new) for d in range(NEW)], axis=0
    )
    high = product.astype(BF16)
    low = (product - high.astype(F32)).astype(BF16)
    new_scores = dot(high, same_head) + dot(low, same_head)
    token_at = iota((BLOCK, local), 0) % NEW
    new_scores = [
        jnp.where(token_at >= d, new_scores[d * BLOCK : (d + 1) * BLOCK, :], NEG_BIG)
        for d in range(NEW)
    ]
    new_peak = functools.reduce(jnp.maximum, new_scores)
    new_weights = [jnp.exp(scores - new_peak) for scores in new_scores]
    new_total = functools.reduce(jnp.add, new_weights)
    new_sum = functools.reduce(
        jnp.add,
        [
            new_weights[d].astype(BF16).astype(F32) * (pltpu.roll(v_new, d, 0) if d else v_new)
            for d in range(NEW)
        ],
    )

    def wait_part(k, carry):
        part_copy(k, lax.rem(me + k, n_seq), lax.rem(me + n_seq - k, n_seq)).wait_recv()
        return carry

    lax.fori_loop(1, n_seq, wait_part, 0)
    lane = iota((128, local), 0)
    column_head = iota((128, local), 1) // HD
    pick_peak = one_hot((lane < 2 * heads) & (lane % heads == column_head))
    pick_total = one_hot(
        (lane >= 2 * heads) & (lane < 4 * heads) & (lane % heads == column_head)
    )
    peaks = dot(got[:, local:], pick_peak).reshape(n_seq, BLOCK, local)
    totals = dot(got[:, local:], pick_total).reshape(n_seq, BLOCK, local)
    sums = got[:, 0:local].astype(F32).reshape(n_seq, BLOCK, local)
    peak = jnp.maximum(jnp.max(peaks, axis=0), new_peak)
    factor = jnp.exp(peaks - peak[None])
    new_factor = jnp.exp(new_peak - peak)
    total = jnp.sum(totals * factor, axis=0) + new_total * new_factor
    weighted = jnp.sum(sums * factor, axis=0) + new_sum * new_factor
    attended = (weighted / total).astype(BF16)

    def tp_copies(stage):
        return [
            pltpu.make_async_remote_copy(
                src_ref=tsend.at[stage],
                dst_ref=trecv.at[stage, k - 1],
                send_sem=tsend_sem.at[stage, k - 1],
                recv_sem=trecv_sem.at[stage, k - 1],
                device_id={"tp": lax.rem(my_tp + k, n_tp)},
                device_id_type=MESH,
            )
            for k in range(1, n_tp)
        ]

    def tp_sum(part, stage):
        tsend[stage] = part.astype(BF16)
        sent = tp_copies(stage)
        for copy in sent:
            copy.start()
        for copy in sent:
            copy.wait()
        for k in range(n_tp - 1):
            part = part + trecv[stage, k].astype(F32)
        return part

    copies[6].wait()
    self_mixed = resid[...] + tp_sum(dot(attended, wso[...]), 0)

    copies[7].wait()
    copies[8].wait()
    cross_normed = layer_norm(self_mixed, gains[1:2, :])
    cross_queries = dot(cross_normed, wcq[...]).astype(BF16).astype(F32) * HD ** (-0.5)
    head_of = iota((BLOCK, local), 1) // HD
    stacked = jnp.concatenate(
        [jnp.where(head_of == h, cross_queries, 0.0) for h in range(heads)], axis=0
    ).astype(BF16)
    sources = enc.shape[2]
    enc_keys = enc[0].reshape(own_requests * sources, local)
    enc_values = enc[1].reshape(own_requests * sources, local)
    cross_scores = dot(stacked, enc_keys, NT)
    shape = cross_scores.shape
    ours = iota(shape, 1) // sources == (iota(shape, 0) % BLOCK) // NEW
    cross_scores = jnp.where(ours, cross_scores, NEG_BIG)
    cross_exp = jnp.exp(cross_scores - jnp.max(cross_scores, axis=-1, keepdims=True))
    cross_probs = (cross_exp / jnp.sum(cross_exp, axis=-1, keepdims=True)).astype(BF16)
    mixed = dot(cross_probs, enc_values)
    context = mixed[0:BLOCK, :]
    for h in range(1, heads):
        context = jnp.where(head_of == h, mixed[h * BLOCK : (h + 1) * BLOCK, :], context)
    copies[9].wait()
    cross_mixed = self_mixed + tp_sum(dot(context.astype(BF16), wco[...]), 1)

    resid[...] = cross_mixed
    last_normed = layer_norm(cross_mixed, gains[2:3, :])
    copies[10].wait()
    units = jnp.maximum(dot(last_normed, wup[...]), 0.0).astype(BF16)
    copies[11].wait()
    down = dot(units, wdn[...])
    for t in range(n_tp):
        dsend[t] = down[:, t * local : (t + 1) * local]
    sent = []
    for k in range(1, n_tp):
        target = lax.rem(my_tp + k, n_tp)
        sent.append(
            pltpu.make_async_remote_copy(
                src_ref=dsend.at[target],
                dst_ref=drecv.at[k - 1],
                send_sem=tsend_sem.at[2, k - 1],
                recv_sem=trecv_sem.at[2, k - 1],
                device_id={"tp": target},
                device_id_type=MESH,
            )
        )
    for copy in sent:
        copy.start()
    total = resid[:, pl.ds(pl.multiple_of(my_tp * local, 128), local)] + dsend[my_tp]
    for k, copy in enumerate(sent):
        copy.wait()
        total = total + drecv[k]
    out_ref[...] = total[0:own_rows, :].astype(BF16)

    def wait_sends(k, carry):
        query_copy(k, me).wait_send()
        part_copy(k, lax.rem(me + k, n_seq), me).wait_send()
        return carry

    lax.fori_loop(1, n_seq, wait_sends, 0)


def solution(mesh):
    n_seq = mesh.shape["seq"]
    n_tp = mesh.shape["tp"]

    def per_device(
        hidden,
        norm_gains,
        w_qkv,
        w_self_out,
        w_cross_q,
        w_cross_out,
        w_up,
        w_down,
        kv_cache,
        encoder_kv,
        cache_lengths,
        page_table,
        group_of,
    ):
        own_rows, width = hidden.shape
        local = w_self_out.shape[0]
        heads = local // HD
        slots = kv_cache.shape[1]
        requests, most_pages = page_table.shape
        group_count = requests // GSIZE
        grows = GSIZE * NEW
        rh = heads * grows
        all_rows = n_seq * BLOCK
        sorted_rows = group_count * grows
        lens = cache_lengths.reshape(1, requests)
        groups = group_of.reshape(1, requests)

        def vmem(shape, dtype):
            return pltpu.VMEM(shape, dtype)

        def like(x, shape=None):
            return pltpu.VMEM(shape or x.shape, x.dtype)

        dma = pltpu.SemaphoreType.DMA
        scratch = [
            like(hidden),
            like(norm_gains),
            like(w_qkv),
            like(w_self_out),
            like(w_cross_q),
            like(w_cross_out),
            like(w_up),
            like(w_down),
            like(kv_cache, kv_cache.shape[1:]),
            like(kv_cache, kv_cache.shape[1:]),
            like(encoder_kv),
            like(lens),
            like(page_table),
            like(groups),
            vmem((BLOCK, width), F32),
            vmem((3, BLOCK, local), BF16),
            vmem((all_rows, local), BF16),
            vmem((most_pages, requests), jnp.int32),
            vmem((most_pages, requests), jnp.int32),
            vmem((slots, requests), jnp.int32),
            vmem((slots, rh), F32),
            vmem((slots, rh), jnp.int32),
            vmem((8, 128), jnp.int32),
            pltpu.SMEM((8, 128), jnp.int32),
            vmem((all_rows, sorted_rows), BF16),
            vmem((sorted_rows, all_rows), BF16),
            vmem((group_count, rh, local), BF16),
            vmem((slots, PAGE, rh), F32),
            vmem((slots, rh), F32),
            vmem((slots, rh), F32),
            vmem((group_count, 8, rh), F32),
            vmem((2, group_count, rh), F32),
            vmem((slots + 1, grows, local), F32),
            vmem((sorted_rows, 4 * rh), BF16),
            vmem((sorted_rows, local + 128), BF16),
            vmem((all_rows, local + 128), BF16),
            vmem((all_rows, local + 128), BF16),
            vmem((2, BLOCK, width), BF16),
            vmem((2, n_tp - 1, BLOCK, width), BF16),
            vmem((n_tp, BLOCK, local), F32),
            vmem((n_tp - 1, BLOCK, local), F32),
            dma((12,)),
            dma((2, 4)),
            dma,
            dma((n_seq,)),
            dma((n_seq,)),
            dma((n_seq,)),
            dma((n_seq,)),
            dma((3, n_tp - 1)),
            dma((3, n_tp - 1)),
        ]
        return pl.pallas_call(
            functools.partial(kernel, n_seq, n_tp),
            out_shape=jax.ShapeDtypeStruct((own_rows, local), BF16),
            in_specs=[pl.BlockSpec(memory_space=pl.ANY)] * 13,
            out_specs=pl.BlockSpec(memory_space=pltpu.VMEM),
            scratch_shapes=scratch,
            compiler_params=pltpu.CompilerParams(
                collective_id=0, has_side_effects=True, vmem_limit_bytes=60 << 20
            ),
        )(
            hidden,
            norm_gains,
            w_qkv,
            w_self_out,
            w_cross_q,
            w_cross_out,
            w_up,
            w_down,
            kv_cache,
            encoder_kv,
            lens,
            page_table,
            groups,
        )

    in_specs = (
        P("seq", None),
        P(),
        P(None, None, "tp"),
        P("tp", None),
        P(None, "tp"),
        P("tp", None),
        P(None, "tp"),
        P("tp", None),
        P(None, "seq", None, "tp"),
        P(None, "seq", None, "tp"),
        P(),
        P(),
        P(),
    )
    return jax.shard_map(
        per_device, mesh=mesh, in_specs=in_specs, out_specs=P("seq", "tp"), check_vma=False
    )
```

```python
import functools

import jax
import jax.numpy as jnp
from jax import lax
from jax.experimental import pallas as pl
from jax.experimental.pallas import tpu as pltpu
from jax.sharding import PartitionSpec as P

HD = 64
PAGE = 128
NEW = 4
GSIZE = 8
BLOCK = 16
NEG_BIG = -1e30
FLOOR = -1e29
MESH = pl.DeviceIdType.MESH
F32 = jnp.float32
BF16 = jnp.bfloat16
NT = (((1,), (1,)), ((), ()))
TN = (((0,), (0,)), ((), ()))


def iota(shape, dim):
    return lax.broadcasted_iota(jnp.int32, shape, dim)


def dot(a, b, dims=None):
    if dims is None:
        return jnp.dot(a, b, preferred_element_type=F32)
    return lax.dot_general(a, b, dims, preferred_element_type=F32)


def layer_norm(values, gain):
    centre = values - jnp.mean(values, axis=-1, keepdims=True)
    spread = jnp.mean(centre * centre, axis=-1, keepdims=True)
    return (centre * lax.rsqrt(spread + 1e-05) * gain).astype(BF16)


def partners(me, n_seq):
    side = 4 if n_seq % 32 == 0 else 1
    depth = n_seq // (2 * side)
    x, z, core = me // (2 * depth), (me // 2) % depth, me % 2

    def turn(at, by, size):
        return jnp.where(at + by >= size, at + by - size, at + by)

    def hops(offset):
        dx, dz, _ = offset
        return min(dx, side - dx) + min(dz, depth - dz)

    offsets = [(dx, dz, dc) for dx in range(side) for dz in range(depth) for dc in range(2)][1:]
    found = []
    for dx, dz, dc in sorted(offsets, key=lambda offset: -hops(offset)):
        c = 1 - core if dc else core
        to = (turn(x, dx, side) * depth + turn(z, dz, depth)) * 2 + c
        back = (turn(x, (side - dx) % side, side) * depth + turn(z, (depth - dz) % depth, depth)) * 2 + c
        found.append((to, back))
    return found


def one_hot(condition):
    return jnp.where(condition, 1.0, 0.0).astype(BF16)


def kernel(
    n_seq,
    n_tp,
    hidden_h,
    gains_h,
    wqkv_h,
    wso_h,
    wcq_h,
    wco_h,
    wup_h,
    wdn_h,
    kv_h,
    enc_h,
    len_h,
    table_h,
    group_h,
    out_ref,
    hidden,
    gains,
    wqkv,
    wso,
    wcq,
    wco,
    wup,
    wdn,
    kbuf,
    vbuf,
    enc,
    lens,
    table,
    groups,
    resid,
    own,
    qall,
    table_t,
    nvalid_t,
    owners,
    nrh,
    gmat,
    scal_v,
    scal_s,
    to_dest,
    to_group,
    qbd,
    sbuf,
    mbuf,
    lbuf,
    mg,
    mparts,
    acc,
    mlsrc,
    paysrc,
    pay,
    got,
    tsend,
    trecv,
    dsend,
    drecv,
    load_sem,
    cache_sem,
    scal_sem,
    qsend_sem,
    qrecv_sem,
    psend_sem,
    precv_sem,
    tsend_sem,
    trecv_sem,
):
    own_rows, width = hidden.shape
    local = wso.shape[0]
    heads = local // HD
    slots = kbuf.shape[0]
    requests = groups.shape[1]
    group_count = requests // GSIZE
    own_requests = own_rows // NEW
    most_pages = table.shape[1]
    grows = GSIZE * NEW
    rh = heads * grows
    all_rows = n_seq * BLOCK
    sorted_rows = group_count * grows
    me = lax.axis_index("seq")
    my_tp = lax.axis_index("tp")
    seq_partners = partners(me, n_seq)
    tp_steps = sorted(range(1, n_tp), key=lambda k: -min(k, n_tp - k))

    loads = [
        (hidden_h, hidden),
        (gains_h, gains),
        (wqkv_h, wqkv),
        (table_h, table),
        (len_h, lens),
        (group_h, groups),
        (wso_h, wso),
        (wcq_h, wcq),
        (enc_h, enc),
        (wco_h, wco),
        (wup_h, wup),
        (wdn_h, wdn),
    ]
    copies = [
        pltpu.make_async_copy(src, dst, load_sem.at[i]) for i, (src, dst) in enumerate(loads)
    ]
    parts = 4
    span = slots // parts
    cache_copies = [
        pltpu.make_async_copy(
            kv_h.at[which, pl.ds(p * span, span)],
            buf.at[pl.ds(p * span, span)],
            cache_sem.at[which, p],
        )
        for which, buf in ((0, kbuf), (1, vbuf))
        for p in range(parts)
    ]
    for copy in copies[:6]:
        copy.start()

    barrier = pltpu.get_barrier_semaphore()

    for target, _ in seq_partners:
        pl.semaphore_signal(barrier, inc=1, device_id={"seq": target}, device_id_type=MESH)
    for k in tp_steps:
        pl.semaphore_signal(
            barrier, inc=1, device_id={"tp": lax.rem(my_tp + k, n_tp)}, device_id_type=MESH
        )

    for copy in cache_copies[:parts]:
        copy.start()
    for copy in cache_copies[parts:]:
        copy.start()
    for copy in copies[6:]:
        copy.start()

    copies[0].wait()
    copies[1].wait()
    resid[...] = jnp.zeros_like(resid)
    resid[0:own_rows, :] = hidden[...].astype(F32)
    normed = layer_norm(resid[...], gains[0:1, :])
    copies[2].wait()
    queries = dot(normed, wqkv[0]).astype(BF16)
    qall[pl.ds(me * BLOCK, BLOCK), :] = queries
    own[0] = queries
    pl.semaphore_wait(barrier, n_seq + n_tp - 2)

    def query_copy(k, target, source):
        return pltpu.make_async_remote_copy(
            src_ref=own.at[0],
            dst_ref=qall.at[pl.ds(source * BLOCK, BLOCK), :],
            send_sem=qsend_sem.at[k],
            recv_sem=qrecv_sem.at[k],
            device_id={"seq": target},
            device_id_type=MESH,
        )

    for k, (target, _) in enumerate(seq_partners):
        query_copy(k, target, me).start()
    own[1] = dot(normed, wqkv[1]).astype(BF16)
    own[2] = dot(normed, wqkv[2]).astype(BF16)

    copies[3].wait()
    copies[4].wait()
    copies[5].wait()
    first_slot = me * slots
    eye = iota((requests, requests), 0) == iota((requests, requests), 1)
    group_row = groups[...]
    group_sq = jnp.broadcast_to(group_row, (requests, requests))
    group_col = jnp.sum(jnp.where(eye, group_sq, 0), axis=1, keepdims=True)
    earlier = iota((requests, requests), 0) < iota((requests, requests), 1)
    same = group_col == group_sq
    member_row = jnp.sum(jnp.where(same & earlier, 1, 0), axis=0, keepdims=True)
    member_sq = jnp.broadcast_to(member_row, (requests, requests))
    member_col = jnp.sum(jnp.where(eye, member_sq, 0), axis=1, keepdims=True)
    place_row = group_row * GSIZE + member_row
    place_col = group_col * GSIZE + member_col
    dest = iota((all_rows, requests), 0)
    inner = dest % BLOCK
    request_of = (dest // BLOCK) * own_requests + inner // NEW
    hit = (request_of == iota((all_rows, requests), 1)) & (inner < own_rows)
    at_col = jnp.sum(jnp.where(hit, place_row + 1, 0), axis=1, keepdims=True)
    token = iota((all_rows, 1), 0) % NEW
    at_col = jnp.where(at_col > 0, (at_col - 1) * NEW + token, -1)
    dest_t = iota((requests, all_rows), 1)
    inner_t = dest_t % BLOCK
    request_t = (dest_t // BLOCK) * own_requests + inner_t // NEW
    hit_t = (request_t == iota((requests, all_rows), 0)) & (inner_t < own_rows)
    at_row = jnp.sum(jnp.where(hit_t, place_col + 1, 0), axis=0, keepdims=True)
    token_t = iota((1, all_rows), 1) % NEW
    at_row = jnp.where(at_row > 0, (at_row - 1) * NEW + token_t, -1)
    to_dest[...] = one_hot(at_col == iota((all_rows, sorted_rows), 1))
    to_group[...] = one_hot(at_row == iota((sorted_rows, all_rows), 0))

    table_t[...] = jnp.transpose(table[...] - first_slot)
    page_at = iota((most_pages, requests), 0)
    nvalid_t[...] = jnp.clip(lens[...] - page_at * PAGE, 0, PAGE)
    unroll = 8

    def match(i, carry):
        slot0 = i * unroll

        def over_pages(j, sums):
            rows = pl.ds(pl.multiple_of(j * 8, 8), 8)
            at = table_t[rows, :]
            count = nvalid_t[rows, :]
            return tuple(jnp.where(at == slot0 + u, count, sums[u]) for u in range(unroll))

        sums = lax.fori_loop(
            0,
            most_pages // 8,
            over_pages,
            tuple(jnp.zeros((8, requests), jnp.int32) for _ in range(unroll)),
            unroll=4,
        )
        for u in range(unroll):
            owners[pl.ds(slot0 + u, 1), :] = jnp.max(sums[u], axis=0, keepdims=True)
        return carry

    lax.fori_loop(0, slots // unroll, match, 0)
    owner = owners[...]
    lane_member = (iota((requests, rh), 1) % grows) // NEW
    nrh[...] = dot(owner.astype(F32).astype(BF16), one_hot(member_col == lane_member))
    slot_group = jnp.max(jnp.where(owner > 0, group_row, -1), axis=1, keepdims=True)
    gmat[...] = jnp.broadcast_to(slot_group, (slots, rh))
    eye_s = iota((slots, slots), 0) == iota((slots, slots), 1)
    group_at = jnp.sum(
        jnp.where(eye_s, jnp.broadcast_to(slot_group, (slots, slots)), 0), axis=0, keepdims=True
    )
    before = (iota((slots, slots), 0) < iota((slots, slots), 1)) & (slot_group == group_at)
    before = before & (slot_group >= 0)
    previous = jnp.max(jnp.where(before, iota((slots, slots), 0), -1), axis=0, keepdims=True)
    mine = slot_group == iota((slots, 128), 1)
    last = jnp.max(jnp.where(mine, iota((slots, 128), 0), -1), axis=0, keepdims=True)
    scal_v[...] = jnp.zeros_like(scal_v)
    scal_v[0:1, 0:slots] = jnp.clip(group_at, 0, group_count - 1)
    scal_v[1:2, 0:slots] = jnp.where(previous < 0, slots, previous)
    scal_v[2:3, :] = jnp.where(last < 0, slots, last)
    scalars = pltpu.make_async_copy(scal_v, scal_s, scal_sem)
    scalars.start()

    for k, (target, source) in enumerate(seq_partners):
        query_copy(k, target, source).wait_recv()
    sorted_queries = dot(to_group[...], qall[...]) * HD ** (-0.5)
    row_head = iota((grows, local), 1) // HD
    for g in range(group_count):
        block = sorted_queries[g * grows : (g + 1) * grows, :]
        for h in range(heads):
            qbd[g, h * grows : (h + 1) * grows, :] = jnp.where(row_head == h, block, 0.0).astype(
                BF16
            )
    scalars.wait()

    for copy in cache_copies[:parts]:
        copy.wait()
    key_at = iota((PAGE, rh), 0).astype(F32)
    step = 32 if slots % 32 == 0 else 16

    def group_of_slot(s):
        return jnp.clip(scal_s[0, s], 0, group_count - 1)

    def acc_slot(row, at):
        return jnp.clip(scal_s[row, at], 0, slots)

    def score(i, carry):
        for u in range(step):
            s = i * step + u
            scores = dot(kbuf[s], qbd[group_of_slot(s)], NT)
            scores = jnp.where(key_at < nrh[pl.ds(s, 1), :], scores, NEG_BIG)
            sbuf[s] = scores
            mbuf[pl.ds(s, 1), :] = jnp.max(scores, axis=0, keepdims=True)
        return carry

    lax.fori_loop(0, slots // step, score, 0)
    for g in range(group_count):
        peak = jnp.max(jnp.where(gmat[...] == g, mbuf[...], NEG_BIG), axis=0, keepdims=True)
        peak = jnp.maximum(peak, FLOOR)
        high = peak.astype(BF16)
        low = (peak - high.astype(F32)).astype(BF16)
        mparts[0, g : g + 1, :] = high.astype(F32)
        mparts[1, g : g + 1, :] = low.astype(F32)
        mg[g] = jnp.broadcast_to(high.astype(F32) + low.astype(F32), (8, rh))

    for copy in cache_copies[parts:]:
        copy.wait()
    acc[slots] = jnp.zeros((grows, local), F32)

    def weigh(i, carry):
        for u in range(step):
            s = i * step + u
            peak = mg[group_of_slot(s)][0:1, :]
            weights = jnp.exp(sbuf[s] - peak)
            lbuf[pl.ds(s, 1), :] = jnp.sum(weights, axis=0, keepdims=True)
            product = dot(weights.astype(BF16), vbuf[s], TN)
            picked = product[0:grows, :]
            for h in range(1, heads):
                picked = jnp.where(row_head == h, product[h * grows : (h + 1) * grows, :], picked)
            acc[s] = picked + acc[acc_slot(1, s)]
        return carry

    lax.fori_loop(0, slots // step, weigh, 0)

    diagonal = (iota((grows, rh), 1) % grows) == iota((grows, rh), 0)
    for g in range(group_count):
        rows = slice(g * grows, (g + 1) * grows)
        total = jnp.sum(jnp.where(gmat[...] == g, lbuf[...], 0.0), axis=0, keepdims=True)
        high = total.astype(BF16).astype(F32)
        pieces = (mparts[0, g : g + 1, :], mparts[1, g : g + 1, :], high, total - high)
        for p, piece in enumerate(pieces):
            mlsrc[rows, p * rh : (p + 1) * rh] = jnp.where(diagonal, piece, 0.0).astype(BF16)
        paysrc[rows, 0:local] = acc[acc_slot(2, g)].astype(BF16)
    per_part = BLOCK * heads
    source = iota((4 * rh, local), 0)
    lane = iota((4 * rh, local), 1)
    spread = one_hot(
        (lane // per_part == source // rh) & (lane % heads == (source % rh) // grows)
    )
    paysrc[:, local:] = dot(mlsrc[...], spread).astype(BF16)
    both = dot(to_dest[...], paysrc[...])
    row_in = iota((BLOCK, local), 0)
    own_lane = ((iota((BLOCK, local), 1) % per_part) // heads == row_in)[None]
    small = jnp.where(own_lane, both[:, local:].reshape(n_seq, BLOCK, local), 0.0)
    small = jnp.sum(small, axis=1, keepdims=True)
    large = both[:, 0:local].reshape(n_seq, BLOCK, local)
    filled = jnp.where((row_in == own_rows)[None], small, large)
    pay[...] = filled.reshape(all_rows, local).astype(BF16)
    got[pl.ds(me * BLOCK, BLOCK), :] = pay[pl.ds(me * BLOCK, BLOCK), :]

    def part_copy(k, target, source):
        return pltpu.make_async_remote_copy(
            src_ref=pay.at[pl.ds(target * BLOCK, BLOCK), :],
            dst_ref=got.at[pl.ds(source * BLOCK, BLOCK), :],
            send_sem=psend_sem.at[k],
            recv_sem=precv_sem.at[k],
            device_id={"seq": target},
            device_id_type=MESH,
        )

    for k, (target, _) in enumerate(seq_partners):
        part_copy(k, target, me).start()

    q_new = own[0].astype(F32) * HD ** (-0.5)
    k_new = own[1].astype(F32)
    v_new = own[2].astype(F32)
    same_head = one_hot(iota((local, local), 0) // HD == iota((local, local), 1) // HD)
    product = jnp.concatenate(
        [q_new * (pltpu.roll(k_new, d, 0) if d else k_new) for d in range(NEW)], axis=0
    )
    high = product.astype(BF16)
    low = (product - high.astype(F32)).astype(BF16)
    new_scores = dot(high, same_head) + dot(low, same_head)
    token_at = iota((BLOCK, local), 0) % NEW
    new_scores = [
        jnp.where(token_at >= d, new_scores[d * BLOCK : (d + 1) * BLOCK, :], NEG_BIG)
        for d in range(NEW)
    ]
    new_peak = functools.reduce(jnp.maximum, new_scores)
    new_weights = [jnp.exp(scores - new_peak) for scores in new_scores]
    new_total = functools.reduce(jnp.add, new_weights)
    new_sum = functools.reduce(
        jnp.add,
        [
            new_weights[d].astype(BF16).astype(F32) * (pltpu.roll(v_new, d, 0) if d else v_new)
            for d in range(NEW)
        ],
    )

    for k, (target, source) in enumerate(seq_partners):
        part_copy(k, target, source).wait_recv()
    sums = got[...].astype(F32).reshape(n_seq, BLOCK, local)
    small = jnp.where(own_lane, sums[:, own_rows : own_rows + 1, :], 0.0)
    small = small.reshape(all_rows, local).astype(BF16)
    lane = iota((local, local), 0)
    column_head = lane % heads == iota((local, local), 1) // HD
    pick_peak = one_hot((lane < 2 * per_part) & column_head)
    pick_total = one_hot((lane >= 2 * per_part) & column_head)
    peaks = dot(small, pick_peak).reshape(n_seq, BLOCK, local)
    totals = dot(small, pick_total).reshape(n_seq, BLOCK, local)
    peak = jnp.maximum(jnp.max(peaks, axis=0), new_peak)
    factor = jnp.exp(peaks - peak[None])
    new_factor = jnp.exp(new_peak - peak)
    total = jnp.sum(totals * factor, axis=0) + new_total * new_factor
    weighted = jnp.sum(sums * factor, axis=0) + new_sum * new_factor
    attended = jnp.where(row_in < own_rows, weighted / total, 0.0).astype(BF16)

    def tp_copies(stage):
        return [
            pltpu.make_async_remote_copy(
                src_ref=tsend.at[stage],
                dst_ref=trecv.at[stage, k - 1],
                send_sem=tsend_sem.at[stage, k - 1],
                recv_sem=trecv_sem.at[stage, k - 1],
                device_id={"tp": lax.rem(my_tp + k, n_tp)},
                device_id_type=MESH,
            )
            for k in tp_steps
        ]

    def tp_sum(part, stage):
        tsend[stage] = part.astype(BF16)
        sent = tp_copies(stage)
        for copy in sent:
            copy.start()
        for copy in sent:
            copy.wait()
        for k in range(n_tp - 1):
            part = part + trecv[stage, k].astype(F32)
        return part

    copies[6].wait()
    self_mixed = resid[...] + tp_sum(dot(attended, wso[...]), 0)

    copies[7].wait()
    copies[8].wait()
    cross_normed = layer_norm(self_mixed, gains[1:2, :])
    cross_queries = dot(cross_normed, wcq[...]).astype(BF16).astype(F32) * HD ** (-0.5)
    head_of = iota((BLOCK, local), 1) // HD
    stacked = jnp.concatenate(
        [jnp.where(head_of == h, cross_queries, 0.0) for h in range(heads)], axis=0
    ).astype(BF16)
    sources = enc.shape[2]
    enc_keys = enc[0].reshape(own_requests * sources, local)
    enc_values = enc[1].reshape(own_requests * sources, local)
    cross_scores = dot(stacked, enc_keys, NT)
    shape = cross_scores.shape
    ours = iota(shape, 1) // sources == (iota(shape, 0) % BLOCK) // NEW
    cross_scores = jnp.where(ours, cross_scores, NEG_BIG)
    cross_exp = jnp.exp(cross_scores - jnp.max(cross_scores, axis=-1, keepdims=True))
    cross_probs = (cross_exp / jnp.sum(cross_exp, axis=-1, keepdims=True)).astype(BF16)
    mixed = dot(cross_probs, enc_values)
    context = mixed[0:BLOCK, :]
    for h in range(1, heads):
        context = jnp.where(head_of == h, mixed[h * BLOCK : (h + 1) * BLOCK, :], context)
    copies[9].wait()
    cross_mixed = self_mixed + tp_sum(dot(context.astype(BF16), wco[...]), 1)

    resid[...] = cross_mixed
    last_normed = layer_norm(cross_mixed, gains[2:3, :])
    copies[10].wait()
    units = jnp.maximum(dot(last_normed, wup[...]), 0.0).astype(BF16)
    copies[11].wait()
    down = dot(units, wdn[...])
    for t in range(n_tp):
        dsend[t] = down[:, t * local : (t + 1) * local].astype(BF16)
    sent = []
    for k in tp_steps:
        target = lax.rem(my_tp + k, n_tp)
        sent.append(
            pltpu.make_async_remote_copy(
                src_ref=dsend.at[target],
                dst_ref=drecv.at[k - 1],
                send_sem=tsend_sem.at[2, k - 1],
                recv_sem=trecv_sem.at[2, k - 1],
                device_id={"tp": target},
                device_id_type=MESH,
            )
        )
    for copy in sent:
        copy.start()
    total = resid[:, pl.ds(pl.multiple_of(my_tp * local, 128), local)] + dsend[my_tp].astype(F32)
    for copy in sent:
        copy.wait()
    for k in range(n_tp - 1):
        total = total + drecv[k].astype(F32)
    out_ref[...] = total[0:own_rows, :].astype(BF16)

    for k, (target, _) in enumerate(seq_partners):
        query_copy(k, target, me).wait_send()
        part_copy(k, target, me).wait_send()


def solution(mesh):
    n_seq = mesh.shape["seq"]
    n_tp = mesh.shape["tp"]

    def per_device(
        hidden,
        norm_gains,
        w_qkv,
        w_self_out,
        w_cross_q,
        w_cross_out,
        w_up,
        w_down,
        kv_cache,
        encoder_kv,
        cache_lengths,
        page_table,
        group_of,
    ):
        own_rows, width = hidden.shape
        local = w_self_out.shape[0]
        heads = local // HD
        slots = kv_cache.shape[1]
        requests, most_pages = page_table.shape
        group_count = requests // GSIZE
        grows = GSIZE * NEW
        rh = heads * grows
        all_rows = n_seq * BLOCK
        sorted_rows = group_count * grows
        lens = cache_lengths.reshape(1, requests)
        groups = group_of.reshape(1, requests)

        def vmem(shape, dtype):
            return pltpu.VMEM(shape, dtype)

        def like(x, shape=None):
            return pltpu.VMEM(shape or x.shape, x.dtype)

        dma = pltpu.SemaphoreType.DMA
        scratch = [
            like(hidden),
            like(norm_gains),
            like(w_qkv),
            like(w_self_out),
            like(w_cross_q),
            like(w_cross_out),
            like(w_up),
            like(w_down),
            like(kv_cache, kv_cache.shape[1:]),
            like(kv_cache, kv_cache.shape[1:]),
            like(encoder_kv),
            like(lens),
            like(page_table),
            like(groups),
            vmem((BLOCK, width), F32),
            vmem((3, BLOCK, local), BF16),
            vmem((all_rows, local), BF16),
            vmem((most_pages, requests), jnp.int32),
            vmem((most_pages, requests), jnp.int32),
            vmem((slots, requests), jnp.int32),
            vmem((slots, rh), F32),
            vmem((slots, rh), jnp.int32),
            vmem((8, 128), jnp.int32),
            pltpu.SMEM((8, 128), jnp.int32),
            vmem((all_rows, sorted_rows), BF16),
            vmem((sorted_rows, all_rows), BF16),
            vmem((group_count, rh, local), BF16),
            vmem((slots, PAGE, rh), F32),
            vmem((slots, rh), F32),
            vmem((slots, rh), F32),
            vmem((group_count, 8, rh), F32),
            vmem((2, group_count, rh), F32),
            vmem((slots + 1, grows, local), F32),
            vmem((sorted_rows, 4 * rh), BF16),
            vmem((sorted_rows, 2 * local), BF16),
            vmem((all_rows, local), BF16),
            vmem((all_rows, local), BF16),
            vmem((2, BLOCK, width), BF16),
            vmem((2, n_tp - 1, BLOCK, width), BF16),
            vmem((n_tp, BLOCK, local), BF16),
            vmem((n_tp - 1, BLOCK, local), BF16),
            dma((12,)),
            dma((2, 4)),
            dma,
            dma((n_seq,)),
            dma((n_seq,)),
            dma((n_seq,)),
            dma((n_seq,)),
            dma((3, n_tp - 1)),
            dma((3, n_tp - 1)),
        ]
        return pl.pallas_call(
            functools.partial(kernel, n_seq, n_tp),
            out_shape=jax.ShapeDtypeStruct((own_rows, local), BF16),
            in_specs=[pl.BlockSpec(memory_space=pl.ANY)] * 13,
            out_specs=pl.BlockSpec(memory_space=pltpu.VMEM),
            scratch_shapes=scratch,
            compiler_params=pltpu.CompilerParams(
                collective_id=0, has_side_effects=True, vmem_limit_bytes=60 << 20
            ),
        )(
            hidden,
            norm_gains,
            w_qkv,
            w_self_out,
            w_cross_q,
            w_cross_out,
            w_up,
            w_down,
            kv_cache,
            encoder_kv,
            lens,
            page_table,
            groups,
        )

    in_specs = (
        P("seq", None),
        P(),
        P(None, None, "tp"),
        P("tp", None),
        P(None, "tp"),
        P("tp", None),
        P(None, "tp"),
        P("tp", None),
        P(None, "seq", None, "tp"),
        P(None, "seq", None, "tp"),
        P(),
        P(),
        P(),
    )
    return jax.shard_map(
        per_device, mesh=mesh, in_specs=in_specs, out_specs=P("seq", "tp"), check_vma=False
    )
```

```python
import functools

import jax
import jax.numpy as jnp
from jax import lax
from jax.experimental import pallas as pl
from jax.experimental.pallas import tpu as pltpu
from jax.sharding import PartitionSpec as P

HD = 64
PAGE = 128
NEW = 4
GSIZE = 8
BLOCK = 16
NEG_BIG = -1e30
FLOOR = -1e29
MESH = pl.DeviceIdType.MESH
F32 = jnp.float32
BF16 = jnp.bfloat16
NT = (((1,), (1,)), ((), ()))
TN = (((0,), (0,)), ((), ()))


def iota(shape, dim):
    return lax.broadcasted_iota(jnp.int32, shape, dim)


def dot(a, b, dims=None):
    if dims is None:
        return jnp.dot(a, b, preferred_element_type=F32)
    return lax.dot_general(a, b, dims, preferred_element_type=F32)


def layer_norm(values, gain):
    centre = values - jnp.mean(values, axis=-1, keepdims=True)
    spread = jnp.mean(centre * centre, axis=-1, keepdims=True)
    return (centre * lax.rsqrt(spread + 1e-05) * gain).astype(BF16)


def partners(me, n_seq):
    side = 4 if n_seq % 32 == 0 else 1
    depth = n_seq // (2 * side)
    x, z, core = me // (2 * depth), (me // 2) % depth, me % 2

    def turn(at, by, size):
        return jnp.where(at + by >= size, at + by - size, at + by)

    def hops(offset):
        dx, dz, _ = offset
        return min(dx, side - dx) + min(dz, depth - dz)

    offsets = [(dx, dz, dc) for dx in range(side) for dz in range(depth) for dc in range(2)][1:]
    found = []
    for dx, dz, dc in sorted(offsets, key=lambda offset: -hops(offset)):
        c = 1 - core if dc else core
        to = (turn(x, dx, side) * depth + turn(z, dz, depth)) * 2 + c
        back = (turn(x, (side - dx) % side, side) * depth + turn(z, (depth - dz) % depth, depth)) * 2 + c
        found.append((to, back))
    return found


def one_hot(condition):
    return jnp.where(condition, 1.0, 0.0).astype(BF16)


def kernel(
    n_seq,
    n_tp,
    hidden_h,
    gains_h,
    wqkv_h,
    wso_h,
    wcq_h,
    wco_h,
    wup_h,
    wdn_h,
    kv_h,
    enc_h,
    len_h,
    table_h,
    group_h,
    out_ref,
    hidden,
    gains,
    wqkv,
    wso,
    wcq,
    wco,
    wup,
    wdn,
    kbuf,
    vbuf,
    enc,
    lens,
    table,
    groups,
    resid,
    own,
    qall,
    table_t,
    nvalid_t,
    owners,
    nrh,
    gmat,
    scal_v,
    scal_s,
    to_dest,
    to_group,
    qbd,
    sbuf,
    mbuf,
    lbuf,
    mg,
    mparts,
    acc,
    mlsrc,
    paysrc,
    pay,
    got,
    tsend,
    trecv,
    dsend,
    drecv,
    load_sem,
    cache_sem,
    scal_sem,
    qsend_sem,
    qrecv_sem,
    psend_sem,
    precv_sem,
    tsend_sem,
    trecv_sem,
):
    own_rows, width = hidden.shape
    local = wso.shape[0]
    heads = local // HD
    slots = kbuf.shape[0]
    requests = groups.shape[1]
    group_count = requests // GSIZE
    own_requests = own_rows // NEW
    most_pages = table.shape[1]
    grows = GSIZE * NEW
    rh = heads * grows
    all_rows = n_seq * BLOCK
    sorted_rows = group_count * grows
    me = lax.axis_index("seq")
    my_tp = lax.axis_index("tp")
    seq_partners = partners(me, n_seq)
    tp_steps = sorted(range(1, n_tp), key=lambda k: -min(k, n_tp - k))

    loads = [
        (hidden_h, hidden),
        (gains_h, gains),
        (wqkv_h, wqkv),
        (table_h, table),
        (len_h, lens),
        (group_h, groups),
        (wso_h, wso),
        (wcq_h, wcq),
        (enc_h, enc),
        (wco_h, wco),
        (wup_h, wup),
        (wdn_h, wdn),
    ]
    copies = [
        pltpu.make_async_copy(src, dst, load_sem.at[i]) for i, (src, dst) in enumerate(loads)
    ]
    parts = 4
    span = slots // parts
    cache_copies = [
        pltpu.make_async_copy(
            kv_h.at[which, pl.ds(p * span, span)],
            buf.at[pl.ds(p * span, span)],
            cache_sem.at[which, p],
        )
        for which, buf in ((0, kbuf), (1, vbuf))
        for p in range(parts)
    ]
    for copy in copies[:6]:
        copy.start()

    barrier = pltpu.get_barrier_semaphore()

    for target, _ in seq_partners:
        pl.semaphore_signal(barrier, inc=1, device_id={"seq": target}, device_id_type=MESH)
    for k in tp_steps:
        pl.semaphore_signal(
            barrier, inc=1, device_id={"tp": lax.rem(my_tp + k, n_tp)}, device_id_type=MESH
        )

    for copy in cache_copies[:parts]:
        copy.start()
    for copy in cache_copies[parts:]:
        copy.start()
    for copy in copies[6:]:
        copy.start()

    copies[0].wait()
    copies[1].wait()
    resid[...] = jnp.zeros_like(resid)
    resid[0:own_rows, :] = hidden[...].astype(F32)
    normed = layer_norm(resid[...], gains[0:1, :])
    copies[2].wait()
    queries = dot(normed, wqkv[0]).astype(BF16)
    qall[pl.ds(me * BLOCK, BLOCK), :] = queries
    own[0] = queries
    pl.semaphore_wait(barrier, n_seq + n_tp - 2)

    def query_copy(k, target, source):
        return pltpu.make_async_remote_copy(
            src_ref=own.at[0],
            dst_ref=qall.at[pl.ds(source * BLOCK, BLOCK), :],
            send_sem=qsend_sem.at[k],
            recv_sem=qrecv_sem.at[k],
            device_id={"seq": target},
            device_id_type=MESH,
        )

    for k, (target, _) in enumerate(seq_partners):
        query_copy(k, target, me).start()
    own[1] = dot(normed, wqkv[1]).astype(BF16)
    own[2] = dot(normed, wqkv[2]).astype(BF16)

    copies[3].wait()
    copies[4].wait()
    copies[5].wait()
    first_slot = me * slots
    eye = iota((requests, requests), 0) == iota((requests, requests), 1)
    group_row = groups[...]
    group_sq = jnp.broadcast_to(group_row, (requests, requests))
    group_col = jnp.sum(jnp.where(eye, group_sq, 0), axis=1, keepdims=True)
    earlier = iota((requests, requests), 0) < iota((requests, requests), 1)
    same = group_col == group_sq
    member_row = jnp.sum(jnp.where(same & earlier, 1, 0), axis=0, keepdims=True)
    member_sq = jnp.broadcast_to(member_row, (requests, requests))
    member_col = jnp.sum(jnp.where(eye, member_sq, 0), axis=1, keepdims=True)
    place_row = group_row * GSIZE + member_row
    place_col = group_col * GSIZE + member_col
    dest = iota((all_rows, requests), 0)
    inner = dest % BLOCK
    request_of = (dest // BLOCK) * own_requests + inner // NEW
    hit = (request_of == iota((all_rows, requests), 1)) & (inner < own_rows)
    at_col = jnp.sum(jnp.where(hit, place_row + 1, 0), axis=1, keepdims=True)
    token = iota((all_rows, 1), 0) % NEW
    at_col = jnp.where(at_col > 0, (at_col - 1) * NEW + token, -1)
    dest_t = iota((requests, all_rows), 1)
    inner_t = dest_t % BLOCK
    request_t = (dest_t // BLOCK) * own_requests + inner_t // NEW
    hit_t = (request_t == iota((requests, all_rows), 0)) & (inner_t < own_rows)
    at_row = jnp.sum(jnp.where(hit_t, place_col + 1, 0), axis=0, keepdims=True)
    token_t = iota((1, all_rows), 1) % NEW
    at_row = jnp.where(at_row > 0, (at_row - 1) * NEW + token_t, -1)
    to_dest[...] = one_hot(at_col == iota((all_rows, sorted_rows), 1))
    to_group[...] = one_hot(at_row == iota((sorted_rows, all_rows), 0))

    table_t[...] = jnp.transpose(table[...] - first_slot)
    page_at = iota((most_pages, requests), 0)
    nvalid_t[...] = jnp.clip(lens[...] - page_at * PAGE, 0, PAGE)
    unroll = 8

    def match(i, carry):
        slot0 = i * unroll

        def over_pages(j, sums):
            rows = pl.ds(pl.multiple_of(j * 8, 8), 8)
            at = table_t[rows, :]
            count = nvalid_t[rows, :]
            return tuple(jnp.where(at == slot0 + u, count, sums[u]) for u in range(unroll))

        sums = lax.fori_loop(
            0,
            most_pages // 8,
            over_pages,
            tuple(jnp.zeros((8, requests), jnp.int32) for _ in range(unroll)),
            unroll=4,
        )
        for u in range(unroll):
            owners[pl.ds(slot0 + u, 1), :] = jnp.max(sums[u], axis=0, keepdims=True)
        return carry

    lax.fori_loop(0, slots // unroll, match, 0)
    owner = owners[...]
    lane_member = (iota((requests, rh), 1) % grows) // NEW
    nrh[...] = dot(owner.astype(F32).astype(BF16), one_hot(member_col == lane_member))
    slot_group = jnp.max(jnp.where(owner > 0, group_row, -1), axis=1, keepdims=True)
    gmat[...] = jnp.broadcast_to(slot_group, (slots, rh))
    eye_s = iota((slots, slots), 0) == iota((slots, slots), 1)
    group_at = jnp.sum(
        jnp.where(eye_s, jnp.broadcast_to(slot_group, (slots, slots)), 0), axis=0, keepdims=True
    )
    before = (iota((slots, slots), 0) < iota((slots, slots), 1)) & (slot_group == group_at)
    before = before & (slot_group >= 0)
    previous = jnp.max(jnp.where(before, iota((slots, slots), 0), -1), axis=0, keepdims=True)
    mine = slot_group == iota((slots, 128), 1)
    last = jnp.max(jnp.where(mine, iota((slots, 128), 0), -1), axis=0, keepdims=True)
    scal_v[...] = jnp.zeros_like(scal_v)
    scal_v[0:1, 0:slots] = jnp.clip(group_at, 0, group_count - 1)
    scal_v[1:2, 0:slots] = jnp.where(previous < 0, slots, previous)
    scal_v[2:3, :] = jnp.where(last < 0, slots, last)
    scalars = pltpu.make_async_copy(scal_v, scal_s, scal_sem)
    scalars.start()

    for k, (target, source) in enumerate(seq_partners):
        query_copy(k, target, source).wait_recv()
    sorted_queries = dot(to_group[...], qall[...]) * HD ** (-0.5)
    row_head = iota((grows, local), 1) // HD
    for g in range(group_count):
        block = sorted_queries[g * grows : (g + 1) * grows, :]
        for h in range(heads):
            qbd[g, h * grows : (h + 1) * grows, :] = jnp.where(row_head == h, block, 0.0).astype(
                BF16
            )
    scalars.wait()

    for copy in cache_copies[:parts]:
        copy.wait()
    key_at = iota((PAGE, rh), 0).astype(F32)
    step = 48 if slots % 48 == 0 else 16

    def group_of_slot(s):
        return jnp.clip(scal_s[0, s], 0, group_count - 1)

    def acc_slot(row, at):
        return jnp.clip(scal_s[row, at], 0, slots)

    def score(i, carry):
        for u in range(step):
            s = i * step + u
            scores = dot(kbuf[s], qbd[group_of_slot(s)], NT)
            scores = jnp.where(key_at < nrh[pl.ds(s, 1), :], scores, NEG_BIG)
            sbuf[s] = scores
            mbuf[pl.ds(s, 1), :] = jnp.max(scores, axis=0, keepdims=True)
        return carry

    lax.fori_loop(0, slots // step, score, 0)
    for g in range(group_count):
        peak = jnp.max(jnp.where(gmat[...] == g, mbuf[...], NEG_BIG), axis=0, keepdims=True)
        peak = jnp.maximum(peak, FLOOR)
        high = peak.astype(BF16)
        low = (peak - high.astype(F32)).astype(BF16)
        mparts[0, g : g + 1, :] = high.astype(F32)
        mparts[1, g : g + 1, :] = low.astype(F32)
        mg[g] = jnp.broadcast_to(high.astype(F32) + low.astype(F32), (8, rh))

    for copy in cache_copies[parts:]:
        copy.wait()
    acc[slots] = jnp.zeros((grows, local), F32)

    def weigh(i, carry):
        for u in range(step):
            s = i * step + u
            peak = mg[group_of_slot(s)][0:1, :]
            weights = jnp.exp(sbuf[s] - peak)
            lbuf[pl.ds(s, 1), :] = jnp.sum(weights, axis=0, keepdims=True)
            product = dot(weights.astype(BF16), vbuf[s], TN)
            picked = product[0:grows, :]
            for h in range(1, heads):
                picked = jnp.where(row_head == h, product[h * grows : (h + 1) * grows, :], picked)
            acc[s] = picked + acc[acc_slot(1, s)]
        return carry

    lax.fori_loop(0, slots // step, weigh, 0)

    diagonal = (iota((grows, rh), 1) % grows) == iota((grows, rh), 0)
    for g in range(group_count):
        rows = slice(g * grows, (g + 1) * grows)
        total = jnp.sum(jnp.where(gmat[...] == g, lbuf[...], 0.0), axis=0, keepdims=True)
        high = total.astype(BF16).astype(F32)
        pieces = (mparts[0, g : g + 1, :], mparts[1, g : g + 1, :], high, total - high)
        for p, piece in enumerate(pieces):
            mlsrc[rows, p * rh : (p + 1) * rh] = jnp.where(diagonal, piece, 0.0).astype(BF16)
        paysrc[rows, 0:local] = acc[acc_slot(2, g)].astype(BF16)
    per_part = BLOCK * heads
    source = iota((4 * rh, local), 0)
    lane = iota((4 * rh, local), 1)
    spread = one_hot(
        (lane // per_part == source // rh) & (lane % heads == (source % rh) // grows)
    )
    paysrc[:, local:] = dot(mlsrc[...], spread).astype(BF16)
    both = dot(to_dest[...], paysrc[...])
    row_in = iota((BLOCK, local), 0)
    own_lane = ((iota((BLOCK, local), 1) % per_part) // heads == row_in)[None]
    small = jnp.where(own_lane, both[:, local:].reshape(n_seq, BLOCK, local), 0.0)
    small = jnp.sum(small, axis=1, keepdims=True)
    large = both[:, 0:local].reshape(n_seq, BLOCK, local)
    filled = jnp.where((row_in == own_rows)[None], small, large)
    pay[...] = filled.reshape(all_rows, local).astype(BF16)
    got[pl.ds(me * BLOCK, BLOCK), :] = pay[pl.ds(me * BLOCK, BLOCK), :]

    def part_copy(k, target, source):
        return pltpu.make_async_remote_copy(
            src_ref=pay.at[pl.ds(target * BLOCK, BLOCK), :],
            dst_ref=got.at[pl.ds(source * BLOCK, BLOCK), :],
            send_sem=psend_sem.at[k],
            recv_sem=precv_sem.at[k],
            device_id={"seq": target},
            device_id_type=MESH,
        )

    for k, (target, _) in enumerate(seq_partners):
        part_copy(k, target, me).start()

    q_new = own[0].astype(F32) * HD ** (-0.5)
    k_new = own[1].astype(F32)
    v_new = own[2].astype(F32)
    same_head = one_hot(iota((local, local), 0) // HD == iota((local, local), 1) // HD)
    product = jnp.concatenate(
        [q_new * (pltpu.roll(k_new, d, 0) if d else k_new) for d in range(NEW)], axis=0
    )
    high = product.astype(BF16)
    low = (product - high.astype(F32)).astype(BF16)
    new_scores = dot(high, same_head) + dot(low, same_head)
    token_at = iota((BLOCK, local), 0) % NEW
    new_scores = [
        jnp.where(token_at >= d, new_scores[d * BLOCK : (d + 1) * BLOCK, :], NEG_BIG)
        for d in range(NEW)
    ]
    new_peak = functools.reduce(jnp.maximum, new_scores)
    new_weights = [jnp.exp(scores - new_peak) for scores in new_scores]
    new_total = functools.reduce(jnp.add, new_weights)
    new_sum = functools.reduce(
        jnp.add,
        [
            new_weights[d].astype(BF16).astype(F32) * (pltpu.roll(v_new, d, 0) if d else v_new)
            for d in range(NEW)
        ],
    )

    for k, (target, source) in enumerate(seq_partners):
        part_copy(k, target, source).wait_recv()
    sums = got[...].astype(F32).reshape(n_seq, BLOCK, local)
    small = jnp.where(own_lane, sums[:, own_rows : own_rows + 1, :], 0.0)
    small = small.reshape(all_rows, local).astype(BF16)
    lane = iota((local, local), 0)
    column_head = lane % heads == iota((local, local), 1) // HD
    pick_peak = one_hot((lane < 2 * per_part) & column_head)
    pick_total = one_hot((lane >= 2 * per_part) & column_head)
    peaks = dot(small, pick_peak).reshape(n_seq, BLOCK, local)
    totals = dot(small, pick_total).reshape(n_seq, BLOCK, local)
    peak = jnp.maximum(jnp.max(peaks, axis=0), new_peak)
    factor = jnp.exp(peaks - peak[None])
    new_factor = jnp.exp(new_peak - peak)
    total = jnp.sum(totals * factor, axis=0) + new_total * new_factor
    weighted = jnp.sum(sums * factor, axis=0) + new_sum * new_factor
    attended = jnp.where(row_in < own_rows, weighted / total, 0.0).astype(BF16)

    def tp_copies(stage):
        return [
            pltpu.make_async_remote_copy(
                src_ref=tsend.at[stage],
                dst_ref=trecv.at[stage, k - 1],
                send_sem=tsend_sem.at[stage, k - 1],
                recv_sem=trecv_sem.at[stage, k - 1],
                device_id={"tp": lax.rem(my_tp + k, n_tp)},
                device_id_type=MESH,
            )
            for k in tp_steps
        ]

    half = width // 2

    def tp_sum(part, stage):
        tsend[stage, 0:own_rows, :] = part[0:own_rows, 0:half].astype(BF16)
        tsend[stage, own_rows : 2 * own_rows, :] = part[0:own_rows, half:].astype(BF16)
        sent = tp_copies(stage)
        for copy in sent:
            copy.start()
        for copy in sent:
            copy.wait()
        others = functools.reduce(
            jnp.add, [trecv[stage, k].astype(F32) for k in range(n_tp - 1)]
        )
        resid[...] += part
        resid[0:own_rows, 0:half] += others[0:own_rows, :]
        resid[0:own_rows, half:] += others[own_rows:, :]
        return resid[...]

    copies[6].wait()
    self_mixed = tp_sum(dot(attended, wso[...]), 0)

    copies[7].wait()
    copies[8].wait()
    cross_normed = layer_norm(self_mixed, gains[1:2, :])
    cross_queries = dot(cross_normed, wcq[...]).astype(BF16).astype(F32) * HD ** (-0.5)
    head_of = iota((BLOCK, local), 1) // HD
    stacked = jnp.concatenate(
        [jnp.where(head_of == h, cross_queries, 0.0) for h in range(heads)], axis=0
    ).astype(BF16)
    sources = enc.shape[2]
    enc_keys = enc[0].reshape(own_requests * sources, local)
    enc_values = enc[1].reshape(own_requests * sources, local)
    cross_scores = dot(stacked, enc_keys, NT)
    shape = cross_scores.shape
    ours = iota(shape, 1) // sources == (iota(shape, 0) % BLOCK) // NEW
    cross_scores = jnp.where(ours, cross_scores, NEG_BIG)
    cross_exp = jnp.exp(cross_scores - jnp.max(cross_scores, axis=-1, keepdims=True))
    cross_probs = (cross_exp / jnp.sum(cross_exp, axis=-1, keepdims=True)).astype(BF16)
    mixed = dot(cross_probs, enc_values)
    context = mixed[0:BLOCK, :]
    for h in range(1, heads):
        context = jnp.where(head_of == h, mixed[h * BLOCK : (h + 1) * BLOCK, :], context)
    copies[9].wait()
    cross_mixed = tp_sum(dot(context.astype(BF16), wco[...]), 1)

    last_normed = layer_norm(cross_mixed, gains[2:3, :])
    copies[10].wait()
    units = jnp.maximum(dot(last_normed, wup[...]), 0.0).astype(BF16)
    copies[11].wait()
    down = dot(units, wdn[...])
    for t in range(n_tp):
        dsend[t] = down[:, t * local : (t + 1) * local].astype(BF16)
    sent = []
    for k in tp_steps:
        target = lax.rem(my_tp + k, n_tp)
        sent.append(
            pltpu.make_async_remote_copy(
                src_ref=dsend.at[target],
                dst_ref=drecv.at[k - 1],
                send_sem=tsend_sem.at[2, k - 1],
                recv_sem=trecv_sem.at[2, k - 1],
                device_id={"tp": target},
                device_id_type=MESH,
            )
        )
    for copy in sent:
        copy.start()
    for k, (target, _) in enumerate(seq_partners):
        query_copy(k, target, me).wait_send()
        part_copy(k, target, me).wait_send()
    total = resid[:, pl.ds(pl.multiple_of(my_tp * local, 128), local)] + dsend[my_tp].astype(F32)
    for copy in sent:
        copy.wait()
    for k in range(n_tp - 1):
        total = total + drecv[k].astype(F32)
    out_ref[...] = total[0:own_rows, :].astype(BF16)


def solution(mesh):
    n_seq = mesh.shape["seq"]
    n_tp = mesh.shape["tp"]

    def per_device(
        hidden,
        norm_gains,
        w_qkv,
        w_self_out,
        w_cross_q,
        w_cross_out,
        w_up,
        w_down,
        kv_cache,
        encoder_kv,
        cache_lengths,
        page_table,
        group_of,
    ):
        own_rows, width = hidden.shape
        local = w_self_out.shape[0]
        heads = local // HD
        slots = kv_cache.shape[1]
        requests, most_pages = page_table.shape
        group_count = requests // GSIZE
        grows = GSIZE * NEW
        rh = heads * grows
        all_rows = n_seq * BLOCK
        sorted_rows = group_count * grows
        lens = cache_lengths.reshape(1, requests)
        groups = group_of.reshape(1, requests)

        def vmem(shape, dtype):
            return pltpu.VMEM(shape, dtype)

        def like(x, shape=None):
            return pltpu.VMEM(shape or x.shape, x.dtype)

        dma = pltpu.SemaphoreType.DMA
        scratch = [
            like(hidden),
            like(norm_gains),
            like(w_qkv),
            like(w_self_out),
            like(w_cross_q),
            like(w_cross_out),
            like(w_up),
            like(w_down),
            like(kv_cache, kv_cache.shape[1:]),
            like(kv_cache, kv_cache.shape[1:]),
            like(encoder_kv),
            like(lens),
            like(page_table),
            like(groups),
            vmem((BLOCK, width), F32),
            vmem((3, BLOCK, local), BF16),
            vmem((all_rows, local), BF16),
            vmem((most_pages, requests), jnp.int32),
            vmem((most_pages, requests), jnp.int32),
            vmem((slots, requests), jnp.int32),
            vmem((slots, rh), F32),
            vmem((slots, rh), jnp.int32),
            vmem((8, 128), jnp.int32),
            pltpu.SMEM((8, 128), jnp.int32),
            vmem((all_rows, sorted_rows), BF16),
            vmem((sorted_rows, all_rows), BF16),
            vmem((group_count, rh, local), BF16),
            vmem((slots, PAGE, rh), F32),
            vmem((slots, rh), F32),
            vmem((slots, rh), F32),
            vmem((group_count, 8, rh), F32),
            vmem((2, group_count, rh), F32),
            vmem((slots + 1, grows, local), F32),
            vmem((sorted_rows, 4 * rh), BF16),
            vmem((sorted_rows, 2 * local), BF16),
            vmem((all_rows, local), BF16),
            vmem((all_rows, local), BF16),
            vmem((2, 2 * own_rows, width // 2), BF16),
            vmem((2, n_tp - 1, 2 * own_rows, width // 2), BF16),
            vmem((n_tp, BLOCK, local), BF16),
            vmem((n_tp - 1, BLOCK, local), BF16),
            dma((12,)),
            dma((2, 4)),
            dma,
            dma((n_seq,)),
            dma((n_seq,)),
            dma((n_seq,)),
            dma((n_seq,)),
            dma((3, n_tp - 1)),
            dma((3, n_tp - 1)),
        ]
        result = pl.pallas_call(
            functools.partial(kernel, n_seq, n_tp),
            out_shape=jax.ShapeDtypeStruct((own_rows, local), BF16),
            in_specs=[pl.BlockSpec(memory_space=pltpu.HBM)] * 13,
            out_specs=pl.BlockSpec(memory_space=pltpu.VMEM),
            scratch_shapes=scratch,
            compiler_params=pltpu.CompilerParams(
                collective_id=0, has_side_effects=True, vmem_limit_bytes=50 << 20
            ),
        )(*[pltpu.with_memory_space_constraint(x, pltpu.HBM) for x in (hidden, norm_gains, w_qkv, w_self_out, w_cross_q, w_cross_out, w_up, w_down, kv_cache, encoder_kv, lens, page_table, groups)])
        return result

    in_specs = (
        P("seq", None),
        P(),
        P(None, None, "tp"),
        P("tp", None),
        P(None, "tp"),
        P("tp", None),
        P(None, "tp"),
        P("tp", None),
        P(None, "seq", None, "tp"),
        P(None, "seq", None, "tp"),
        P(),
        P(),
        P(),
    )
    return jax.shard_map(
        per_device, mesh=mesh, in_specs=in_specs, out_specs=P("seq", "tp"), check_vma=False
    )
```
